32 devices in a mesh: ta: 4 (over y, core), gx: 8 (over z, x).
Axes of the slice: x: 2, y: 2, z: 4, core: 2. Of those that a mesh axis runs over, the one named last changes fastest.
Arguments:
- gauge_links: float32 [4, 2, 3, 3, 8, 32, 256], P(None, None, None, None, 'ta', 'gx'), may hold values from -1 to 1, as said below
Outputs:
- rotated: float32 [4, 2, 3, 3, 8, 32, 256], P(None, None, None, None, 'ta', 'gx')
The draws below stay inside these ranges and needn't reach their ends.
Inputs may be any that keep to these rules, and one draw needn't show every extreme that they name: `gauge_links`: every link is a special unitary 3 x 3 matrix.
All inputs are finite; a program needn't handle non-finite values.
Results may differ from the reference program's by a relative error of at most 0.0003.
Values sent between devices are 32-bit elements; how exact they have to be, the bound alone decides.
No kernel may reach another device: no remote copies, remote signals or barrier semaphores. Data moves between devices by JAX's collectives and lax.ppermute only.
A program may use at most 64 MiB of HBM per device.

```python
import math
import jax
import jax.numpy as jnp
from jax import lax

NY = 16
NZ = 16
NEWTON = 5
NT = 8
NX = 32


def embed_rotation(key, first, second, base_shape):
    key_alpha, key_beta, key_theta = jax.random.split(key, 3)
    alpha = jax.random.uniform(key_alpha, base_shape, jnp.float32, -math.pi, math.pi)
    beta = jax.random.uniform(key_beta, base_shape, jnp.float32, -math.pi, math.pi)
    theta = jax.random.uniform(key_theta, base_shape, jnp.float32, 0.0, 0.5 * math.pi)
    zeros = jnp.zeros(base_shape, jnp.float32)
    ones = jnp.ones(base_shape, jnp.float32)
    real_rows = [[ones if row == col else zeros for col in range(3)] for row in range(3)]
    imag_rows = [[zeros for col in range(3)] for row in range(3)]
    cos_t = jnp.cos(theta)
    sin_t = jnp.sin(theta)
    real_rows[first][first] = jnp.cos(alpha) * cos_t
    imag_rows[first][first] = jnp.sin(alpha) * cos_t
    real_rows[first][second] = jnp.cos(beta) * sin_t
    imag_rows[first][second] = jnp.sin(beta) * sin_t
    real_rows[second][first] = -jnp.cos(beta) * sin_t
    imag_rows[second][first] = jnp.sin(beta) * sin_t
    real_rows[second][second] = jnp.cos(alpha) * cos_t
    imag_rows[second][second] = -jnp.sin(alpha) * cos_t
    return (real_rows, imag_rows)


def multiply_lists(left_pair, right_pair):
    left_re, left_im = left_pair
    right_re, right_im = right_pair
    out_re = [[None] * 3 for row in range(3)]
    out_im = [[None] * 3 for row in range(3)]
    for row in range(3):
        for col in range(3):
            acc_re = left_re[row][0] * right_re[0][col] - left_im[row][0] * right_im[0][col]
            acc_im = left_re[row][0] * right_im[0][col] + left_im[row][0] * right_re[0][col]
            for inner in (1, 2):
                acc_re = acc_re + left_re[row][inner] * right_re[inner][col] - left_im[row][inner] * right_im[inner][col]
                acc_im = acc_im + left_re[row][inner] * right_im[inner][col] + left_im[row][inner] * right_re[inner][col]
            out_re[row][col] = acc_re
            out_im[row][col] = acc_im
    return (out_re, out_im)


def draw_gauge_links(key, part):
    base_shape = (4, NT, NX, NY * NZ)
    key_one, key_two, key_three = jax.random.split(jax.random.fold_in(key, 17), 3)
    first_rot = embed_rotation(key_one, 0, 1, base_shape)
    second_rot = embed_rotation(key_two, 1, 2, base_shape)
    third_rot = embed_rotation(key_three, 0, 2, base_shape)
    whole_re, whole_im = multiply_lists(multiply_lists(first_rot, second_rot), third_rot)
    real_all = jnp.stack([jnp.stack(whole_re[row], 1) for row in range(3)], 1)
    imag_all = jnp.stack([jnp.stack(whole_im[row], 1) for row in range(3)], 1)
    return jnp.stack([real_all, imag_all], axis=1)


def setup_inputs(seed: int = 0) -> dict:
    arg_keys = jax.random.split(jax.random.key(seed), 2)
    return {
        "gauge_links": draw_gauge_links(jax.random.fold_in(arg_keys[1], 71), 0),
    }


ape_weight = 0.4

def matmul_pair(left_mat, right_mat):
    real_part = left_mat[0][:, 0, None] * right_mat[0][None, 0] - left_mat[1][:, 0, None] * right_mat[1][None, 0]
    imag_part = left_mat[0][:, 0, None] * right_mat[1][None, 0] + left_mat[1][:, 0, None] * right_mat[0][None, 0]
    for column in (1, 2):
        real_part = real_part + left_mat[0][:, column, None] * right_mat[0][None, column] - left_mat[1][:, column, None] * right_mat[1][None, column]
        imag_part = imag_part + left_mat[0][:, column, None] * right_mat[1][None, column] + left_mat[1][:, column, None] * right_mat[0][None, column]
    return jnp.stack([real_part, imag_part])

def dagger_of(matrix):
    return jnp.stack([jnp.swapaxes(matrix[0], 0, 1), -jnp.swapaxes(matrix[1], 0, 1)])

def identity_like(template):
    tail = template.shape[3:]
    real_part = jnp.broadcast_to(jnp.eye(3, dtype=jnp.float32).reshape((3, 3) + (1,) * len(tail)), (3, 3) + tail)
    return jnp.stack([real_part, jnp.zeros_like(real_part)])

def yz_roll(source, shift_y, shift_z):
    if shift_y == 0 and shift_z == 0:
        return source
    dims_now = source.shape
    plane = source.reshape(dims_now[:-1] + (NY, NZ))
    plane = jnp.roll(plane, (-shift_y, -shift_z), axis=(-2, -1))
    return plane.reshape(dims_now)

def shifted(source, offset):
    moved_part = jnp.roll(source, (-offset[0], -offset[1]), axis=(-3, -2))
    return yz_roll(moved_part, offset[2], offset[3])

def unit_offset(direction):
    return tuple((1 if axis_pos == direction else 0 for axis_pos in range(4)))

def unitarise(blended):
    three_eye = 3.0 * identity_like(blended)
    frobenius = jnp.sqrt(lax.optimization_barrier(jnp.sum(blended * blended, axis=(0, 1, 2))))
    current = blended / jnp.maximum(frobenius, 1.0)
    for repeat in range(NEWTON):
        current = 0.5 * matmul_pair(current, three_eye - matmul_pair(dagger_of(current), current))
    return current

def smear(gauge_links, mover):
    result = []
    anchor = (0, 0, 0, 0)
    for direction in range(4):
        step_dir = unit_offset(direction)
        staple_sum = None
        for other in range(4):
            if other == direction:
                continue
            step_other = unit_offset(other)
            back_other = tuple((-value for value in step_other))
            diagonal_step = tuple((first - second for first, second in zip(step_dir, step_other)))
            upper_path = matmul_pair(matmul_pair(mover(gauge_links[other], anchor), mover(gauge_links[direction], step_other)), dagger_of(mover(gauge_links[other], step_dir)))
            lower_path = matmul_pair(matmul_pair(dagger_of(mover(gauge_links[other], back_other)), mover(gauge_links[direction], back_other)), mover(gauge_links[other], diagonal_step))
            if staple_sum is None:
                staple_sum = upper_path + lower_path
            else:
                staple_sum = staple_sum + upper_path + lower_path
        blended = (1.0 - ape_weight) * mover(gauge_links[direction], anchor) + ape_weight / 6.0 * staple_sum
        result.append(unitarise(blended))
    return jnp.stack(result)

def chain_step(carry_mat, link_now):
    return (matmul_pair(carry_mat, link_now), carry_mat)

def reference(gauge_links):
    current = gauge_links
    for repeat in range(2):
        current = smear(current, shifted)
    temporal = jnp.moveaxis(current[0], 3, 0)
    start = identity_like(temporal[0])
    final, before = lax.scan(chain_step, start, temporal)
    rotation = jnp.moveaxis(before, 0, 3)
    after_rot = jnp.moveaxis(jnp.concatenate([before[1:], final[None]], 0), 0, 3)
    neighbours = [after_rot, jnp.roll(rotation, -1, axis=-2), yz_roll(rotation, 1, 0), yz_roll(rotation, 0, 1)]
    result = []
    for direction in range(4):
        result.append(matmul_pair(matmul_pair(rotation, current[direction]), dagger_of(neighbours[direction])))
    return jnp.stack(result)
```

```python
import functools

import jax
import jax.numpy as jnp
from jax import lax
from jax.experimental import pallas as pl
from jax.experimental.pallas import tpu as pltpu
from jax.sharding import PartitionSpec as P

NZ = 16
NEWTON = 5
LANES = 128
KEEP = 0.6
BLEND = 0.4 / 6.0
T, X, Y, Z = 0, 1, 2, 3
IDX = ((0, 0), (0, 1), (0, 2), (1, 0), (1, 1), (1, 2), (2, 0), (2, 1), (2, 2))
HALO_T = (X, Y, Z)
HALO_X = (T, Y, Z)


def load(ref, lead, h):
    return tuple([[ref[(*lead, part, i, j, h)] for j in range(3)] for i in range(3)] for part in range(2))


def store(ref, lead, h, mat):
    for part in range(2):
        for i, j in IDX:
            ref[(*lead, part, i, j, h)] = mat[part][i][j]


def accumulate(ref, lead, h, mat):
    for part in range(2):
        for i, j in IDX:
            ref[(*lead, part, i, j, h)] += mat[part][i][j]


def each(fn, *mats):
    return tuple([[fn(*[mat[part][i][j] for mat in mats]) for j in range(3)] for i in range(3)] for part in range(2))


def mul(left, right, left_dag=False, right_dag=False):
    out_re = [[None] * 3 for _ in range(3)]
    out_im = [[None] * 3 for _ in range(3)]
    for i, j in IDX:
        acc_re = acc_im = None
        for k in range(3):
            li, lj = (k, i) if left_dag else (i, k)
            ri, rj = (j, k) if right_dag else (k, j)
            a, b = left[0][li][lj], left[1][li][lj]
            c, d = right[0][ri][rj], right[1][ri][rj]
            ac, bd, ad, bc = a * c, b * d, a * d, b * c
            re = ac + bd if left_dag != right_dag else ac - bd
            if left_dag:
                im = ad - bc
            elif right_dag:
                im = bc - ad
            else:
                im = ad + bc
            acc_re = re if acc_re is None else acc_re + re
            acc_im = im if acc_im is None else acc_im + im
        out_re[i][j], out_im[i][j] = acc_re, acc_im
    return out_re, out_im


def third_row(mat):
    (re, im) = mat
    re, im = [re[0], re[1], [None] * 3], [im[0], im[1], [None] * 3]
    for j in range(3):
        u, v = (j + 1) % 3, (j + 2) % 3
        re[2][j] = re[0][u] * re[1][v] - im[0][u] * im[1][v] - re[0][v] * re[1][u] + im[0][v] * im[1][u]
        im[2][j] = re[0][v] * im[1][u] + im[0][v] * re[1][u] - re[0][u] * im[1][v] - im[0][u] * re[1][v]
    return re, im


class Tile:
    def __init__(self, nt, nx, nh):
        self.nt, self.nx, self.nh, self.rows = nt, nx, nh, nt * nx
        shape = (self.rows, LANES)
        self.row = lax.broadcasted_iota(jnp.int32, shape, 0)
        lane = lax.broadcasted_iota(jnp.int32, shape, 1)
        self.z_last = lane % NZ == NZ - 1
        self.z_first = lane % NZ == 0
        self.y_low = lane < LANES - NZ
        self.y_high = lane >= NZ

    def z_up(self, v):
        return jnp.where(self.z_last, pltpu.roll(v, NZ - 1, 1), pltpu.roll(v, LANES - 1, 1))

    def z_down(self, v):
        return jnp.where(self.z_first, pltpu.roll(v, LANES - NZ + 1, 1), pltpu.roll(v, 1, 1))

    def y_up(self, v, following):
        return jnp.where(self.y_low, pltpu.roll(v, LANES - NZ, 1), pltpu.roll(following, LANES - NZ, 1))

    def y_down(self, v, before):
        return jnp.where(self.y_high, pltpu.roll(v, NZ, 1), pltpu.roll(before, NZ, 1))

    def spread(self, halo, col):
        out = jnp.broadcast_to(halo[0:1], (self.rows, LANES))
        for t in range(1, self.nt):
            out = jnp.where(self.row >= t * self.nx, jnp.broadcast_to(halo[t : t + 1], (self.rows, LANES)), out)
        return out

    def col(self, x):
        return self.row % self.nx == x

    def x_up(self, v, halo):
        return jnp.where(self.col(self.nx - 1), halo, pltpu.roll(v, self.rows - 1, 0))

    def x_down(self, v, halo):
        return jnp.where(self.col(0), halo, pltpu.roll(v, 1, 0))

    def t_up(self, v, halo):
        return jnp.concatenate([v[self.nx :], halo], axis=0)

    def t_down(self, v, halo):
        return jnp.concatenate([halo, v[: self.rows - self.nx]], axis=0)

    def take_x(self, v, x):
        return jnp.concatenate([v[t * self.nx + x : t * self.nx + x + 1] for t in range(self.nt)], axis=0)


def up(tile, ref, m, k, h):
    here = load(ref, (m,), h)
    if k == Z:
        return each(tile.z_up, here)
    return each(tile.y_up, here, load(ref, (m,), (h + 1) % tile.nh))


def down(tile, ref, lead, k, h):
    here = load(ref, lead, h)
    if k == Z:
        return each(tile.z_down, here)
    return each(tile.y_down, here, load(ref, lead, (h + tile.nh - 1) % tile.nh))


def load_rows(ref, lead, h, kept):
    mat = tuple([[ref[(*lead, part, i, j, h)] for j in range(3)] for i in range(kept)] for part in range(2))
    return mat if kept == 3 else third_row(mat)


def store_rows(ref, lead, h, mat, kept):
    for part in range(2):
        for i in range(kept):
            for j in range(3):
                ref[(*lead, part, i, j, h)] = mat[part][i][j]


def send_down(tile, site, dt_ref, dx_ref, ct_ref, cx_ref, h, kept):
    nx, last = tile.nx, (tile.nt - 1) * tile.nx
    for m in range(4):
        mat = load(site, (m,), h)
        if m != T:
            store_rows(dt_ref, (m - 1,), h, each(lambda v: v[:nx], mat), kept)
        if m != X:
            store_rows(dx_ref, (HALO_X.index(m),), h, each(lambda v: tile.take_x(v, 0), mat), kept)
        if m == T:
            store_rows(ct_ref, (), h, each(lambda v: v[last : last + 1], mat), kept)
        if m == X:
            store_rows(cx_ref, (), h, each(lambda v: v[nx - 1 : nx], mat), kept)


def pack_kernel(nt, nx, nh, kept, raw, site, dt_ref, dx_ref, ct_ref, cx_ref):
    tile = Tile(nt, nx, nh)
    for h in range(nh):
        for m in range(4):
            for part in range(2):
                for i, j in IDX:
                    for t in range(nt):
                        site[m, part, i, j, h, t * nx : (t + 1) * nx] = raw[m, part, i, j, t, :, h * LANES : (h + 1) * LANES]
        send_down(tile, site, dt_ref, dx_ref, ct_ref, cx_ref, h, kept)


PAIRS = ((T, Y), (T, Z), (X, Y), (X, Z))


def early_kernel(nt, nx, nh, kept, site, ut_ref, ux_ref, part_ref, corner_ref, low_ref, low_yz):
    tile = Tile(nt, nx, nh)
    last = (nt - 1) * nx

    def step(h, _):
        u = functools.partial(load, site, h=h)
        y_of_z = up(tile, site, Z, Y, h)
        z_of_y = up(tile, site, Y, Z, h)
        path = mul(u((Y,)), y_of_z)
        other = mul(u((Z,)), z_of_y)
        store(part_ref, (Z,), h, mul(path, z_of_y, right_dag=True))
        store(part_ref, (Y,), h, mul(other, y_of_z, right_dag=True))
        store(low_yz, (0,), h, mul(u((Y,)), other, left_dag=True))
        store(low_yz, (1,), h, mul(u((Z,)), path, left_dag=True))
        for place, (k, m) in enumerate(PAIRS):
            other = mul(u((m,)), up(tile, site, k, m, h))
            store(corner_ref, (place,), h, other)
            low = mul(u((k,)), other, left_dag=True)
            store(low_ref, (place,), h, low)
            if k == T:
                store_rows(ut_ref, (m - 1,), h, each(lambda v: v[last:], low), kept)
            else:
                store_rows(ux_ref, (HALO_X.index(m),), h, each(lambda v: tile.take_x(v, nx - 1), low), kept)
        turn = mul(u((T,)), u((X,)), left_dag=True)
        store(corner_ref, (4,), h, turn)
        eye_x = tuple(
            [
                [
                    jnp.where(tile.col(nx - 1), 1.0 if part == 0 and i == j else 0.0, pltpu.roll(site[T, part, i, j, h], tile.rows - 1, 0))
                    for j in range(3)
                ]
                for i in range(3)
            ]
            for part in range(2)
        )
        low = mul(turn, eye_x)
        store_rows(ut_ref, (X - 1,), h, each(lambda v: v[last:], low), kept)
        eye_t = tuple(
            [
                [
                    jnp.where(tile.row >= last, 1.0 if part == 0 and i == j else 0.0, pltpu.roll(site[X, part, i, j, h], tile.rows - nx, 0))
                    for j in range(3)
                ]
                for i in range(3)
            ]
            for part in range(2)
        )
        low = mul(turn, eye_t, left_dag=True)
        store_rows(ux_ref, (HALO_X.index(T),), h, each(lambda v: tile.take_x(v, nx - 1), low), kept)
        return 0

    lax.fori_loop(0, nh, step, 0)

    def finish(h, _):
        accumulate(part_ref, (Z,), h, down(tile, low_yz, (0,), Y, h))
        accumulate(part_ref, (Y,), h, down(tile, low_yz, (1,), Z, h))
        return 0

    lax.fori_loop(0, nh, finish, 0)


def middle_kernel(nt, nx, nh, kept, site, part_ref, corner_ref, dt_ref, dx_ref, sum_ref, turn_ref, low_ref):
    tile = Tile(nt, nx, nh)

    def step(h, _):
        u = functools.partial(load, site, h=h)

        def ahead(m, k):
            if k == T:
                return each(tile.t_up, u((m,)), load_rows(dt_ref, (m - 1,), h, kept))
            halo = load_rows(dx_ref, (HALO_X.index(m),), h, kept)
            return each(lambda v, w: tile.x_up(v, tile.spread(w, nx - 1)), u((m,)), halo)

        x_of_t = ahead(T, X)
        t_of_x = ahead(X, T)
        store(sum_ref, (X,), h, mul(mul(u((T,)), t_of_x), x_of_t, right_dag=True))
        store(sum_ref, (T,), h, mul(mul(u((X,)), x_of_t), t_of_x, right_dag=True))
        turn = load(corner_ref, (4,), h)
        store(turn_ref, (0,), h, mul(turn, x_of_t))
        store(turn_ref, (1,), h, mul(turn, t_of_x, left_dag=True))
        for m in (Y, Z):
            store(sum_ref, (m,), h, load(part_ref, (m,), h))
        for place, (k, m) in enumerate(PAIRS):
            k_of_m = ahead(m, k)
            accumulate(sum_ref, (k,), h, mul(load(corner_ref, (place,), h), k_of_m, right_dag=True))
            path = mul(u((k,)), k_of_m)
            accumulate(sum_ref, (m,), h, mul(path, up(tile, site, k, m, h), right_dag=True))
            store(low_ref, (place,), h, mul(u((m,)), path, left_dag=True))
        return 0

    lax.fori_loop(0, nh, step, 0)

    def finish(h, _):
        for place, (k, m) in enumerate(PAIRS):
            accumulate(sum_ref, (k,), h, down(tile, low_ref, (place,), m, h))
        return 0

    lax.fori_loop(0, nh, finish, 0)


def unitarise(v):
    re, im = v
    diag = []
    for i in range(3):
        total = re[0][i] * re[0][i] + im[0][i] * im[0][i]
        for k in (1, 2):
            total = total + re[k][i] * re[k][i] + im[k][i] * im[k][i]
        diag.append(total)
    off = {}
    for i, j in ((0, 1), (0, 2), (1, 2)):
        off_re = re[0][i] * re[0][j] + im[0][i] * im[0][j]
        off_im = re[0][i] * im[0][j] - im[0][i] * re[0][j]
        for k in (1, 2):
            off_re = off_re + re[k][i] * re[k][j] + im[k][i] * im[k][j]
            off_im = off_im + re[k][i] * im[k][j] - im[k][i] * re[k][j]
        off[i, j] = (off_re, off_im)
    square = diag[0] + diag[1] + diag[2]
    bound = jnp.maximum(square, 1.0)
    inverse = lax.rsqrt(bound)
    inverse = inverse * (1.5 - 0.5 * bound * inverse * inverse)
    scale = inverse * inverse
    mean = square * scale * (1.0 / 3.0)
    q0, q1, q2 = (entry * scale - mean for entry in diag)
    ar, ai = (entry * scale for entry in off[0, 1])
    br, bi = (entry * scale for entry in off[0, 2])
    cr, ci = (entry * scale for entry in off[1, 2])
    na, nb, nc = ar * ar + ai * ai, br * br + bi * bi, cr * cr + ci * ci
    s0, s1, s2 = q0 * q0 + na + nb, q1 * q1 + na + nc, q2 * q2 + nb + nc
    sar, sai = br * cr + bi * ci - q2 * ar, bi * cr - br * ci - q2 * ai
    mr, mi = ar * cr - ai * ci, ar * ci + ai * cr
    sbr, sbi = mr - q1 * br, mi - q1 * bi
    scr, sci = ar * br + ai * bi - q0 * cr, ar * bi - ai * br - q0 * ci
    e2 = 0.5 * (s0 + s1 + s2)
    e3 = q0 * (q1 * q2 - nc) - q1 * nb - q2 * na + 2.0 * (mr * br + mi * bi)
    p0, p1, p2 = 1.5 - 0.5 * mean, jnp.full_like(mean, -0.5), jnp.zeros_like(mean)
    for _ in range(NEWTON - 1):
        d0, d1 = p0 + p0, p1 + p1
        t3, t4 = d1 * p2, p2 * p2
        z0 = p0 * p0 + e3 * t3
        z1 = d0 * p1 + e2 * t3 + e3 * t4
        z2 = p1 * p1 + d0 * p2 + e2 * t4
        y0 = 1.5 - 0.5 * (mean * z0 + e3 * z2)
        y1 = -0.5 * (mean * z1 + z0 + e2 * z2)
        y2 = -0.5 * (mean * z2 + z1)
        u3, u4 = p1 * y2 + p2 * y1, p2 * y2
        p0, p1, p2 = (
            p0 * y0 + e3 * u3,
            p0 * y1 + p1 * y0 + e2 * u3 + e3 * u4,
            p0 * y2 + p1 * y1 + p2 * y0 + e2 * u4,
        )
    p0, p1, p2 = p0 * inverse, p1 * inverse, p2 * inverse
    g0, g1, g2 = (p0 + p1 * q + p2 * s for q, s in ((q0, s0), (q1, s1), (q2, s2)))
    gar, gai = p1 * ar + p2 * sar, p1 * ai + p2 * sai
    gbr, gbi = p1 * br + p2 * sbr, p1 * bi + p2 * sbi
    gcr, gci = p1 * cr + p2 * scr, p1 * ci + p2 * sci
    out_re = [[None] * 3 for _ in range(3)]
    out_im = [[None] * 3 for _ in range(3)]
    for i in range(3):
        x0, x1, x2 = re[i]
        w0, w1, w2 = im[i]
        out_re[i][0] = x0 * g0 + x1 * gar + w1 * gai + x2 * gbr + w2 * gbi
        out_im[i][0] = w0 * g0 + w1 * gar - x1 * gai + w2 * gbr - x2 * gbi
        out_re[i][1] = x1 * g1 + x0 * gar - w0 * gai + x2 * gcr + w2 * gci
        out_im[i][1] = w1 * g1 + w0 * gar + x0 * gai + w2 * gcr - x2 * gci
        out_re[i][2] = x2 * g2 + x0 * gbr - w0 * gbi + x1 * gcr - w1 * gci
        out_im[i][2] = w2 * g2 + w0 * gbr + x0 * gbi + w1 * gcr + x1 * gci
    return out_re, out_im


def new_links(tile, kept, m, site, sum_ref, turn_ref, low_ref, ut_ref, ux_ref, ct_ref, cx_ref, h):
    nt, nx = tile.nt, tile.nx
    total = load(sum_ref, (m,), h)
    if m != T:
        source, lead = (turn_ref, (0,)) if m == X else (low_ref, (PAIRS.index((T, m)),))
        halo = load_rows(ut_ref, (m - 1,), h, kept)
        if m == X:
            end = mul(each(lambda v: v[nx - 1 :], halo), load_rows(ct_ref, (), h, kept))
            halo = each(lambda v, w: jnp.concatenate([v[: nx - 1], w], axis=0), halo, end)
        total = each(lambda acc, v, w: acc + tile.t_down(v, w), total, load(source, lead, h), halo)
    if m != X:
        source, lead = (turn_ref, (1,)) if m == T else (low_ref, (PAIRS.index((X, m)),))
        halo = load_rows(ux_ref, (HALO_X.index(m),), h, kept)
        if m == T:
            end = mul(each(lambda v: v[nt - 1 :], halo), load_rows(cx_ref, (), h, kept))
            halo = each(lambda v, w: jnp.concatenate([v[: nt - 1], w], axis=0), halo, end)
        total = each(lambda acc, v, w: acc + tile.x_down(v, tile.spread(w, 0)), total, load(source, lead, h), halo)
    return unitarise(each(lambda a, b: KEEP * a + BLEND * b, load(site, (m,), h), total))


def late_kernel(nt, nx, nh, kept, site, sum_ref, turn_ref, low_ref, ut_ref, ux_ref, ct_ref, cx_ref, out, dt_ref, dx_ref, dct_ref, dcx_ref):
    tile = Tile(nt, nx, nh)

    def step(h, _):
        for m in range(4):
            store(out, (m,), h, new_links(tile, kept, m, site, sum_ref, turn_ref, low_ref, ut_ref, ux_ref, ct_ref, cx_ref, h))
        send_down(tile, out, dt_ref, dx_ref, dct_ref, dcx_ref, h, 3)
        return 0

    lax.fori_loop(0, nh, step, 0)


def time_kernel(nt, nx, nh, kept, site, sum_ref, turn_ref, low_ref, ut_ref, ux_ref, ct_ref, cx_ref, out, prod_ref):
    tile = Tile(nt, nx, nh)

    def step(h, _):
        links = new_links(tile, kept, T, site, sum_ref, turn_ref, low_ref, ut_ref, ux_ref, ct_ref, cx_ref, h)
        store(out, (), h, links)
        run = each(lambda v: v[:nx], links)
        for t in range(1, nt):
            run = mul(run, each(lambda v: v[t * nx : (t + 1) * nx], links))
        store(prod_ref, (), h, run)
        return 0

    lax.fori_loop(0, nh, step, 0)


def space_kernel(nt, nx, nh, kept, site, sum_ref, turn_ref, low_ref, ut_ref, ux_ref, ct_ref, cx_ref, out):
    tile = Tile(nt, nx, nh)

    def step(h, _):
        for m in (X, Y, Z):
            store(out, (m - 1,), h, new_links(tile, kept, m, site, sum_ref, turn_ref, low_ref, ut_ref, ux_ref, ct_ref, cx_ref, h))
        return 0

    lax.fori_loop(0, nh, step, 0)


def gauge_kernel(nt, nx, nh, count, mine, links, *refs):
    earlier, (rot, after, first) = refs[: count - 1], refs[count - 1 :]
    tile = Tile(nt, nx, nh)
    me = mine[0]

    def step(h, _):
        run = None
        for place in reversed(range(count - 1)):
            there = jnp.full((nx, LANES), me, jnp.int32) > place
            mat = load(earlier[place], (), h)
            mat = tuple(
                [[jnp.where(there, mat[part][i][j], 1.0 if part == 0 and i == j else 0.0) for j in range(3)] for i in range(3)]
                for part in range(2)
            )
            run = mat if run is None else mul(run, mat)
        here = load(links, (), h)
        slices = [run]
        for t in range(nt):
            slices.append(mul(slices[-1], each(lambda v: v[t * nx : (t + 1) * nx], here)))
        before = each(lambda *v: jnp.concatenate(v, axis=0), *slices[:-1])
        store(rot, (), h, before)
        store(after, (), h, each(lambda *v: jnp.concatenate(v, axis=0), *slices[1:]))
        store(first, (), h, each(lambda v: tile.take_x(v, 0), before))
        return 0

    lax.fori_loop(0, nh, step, 0)


def put_raw(nt, nx, raw, m, h, mat):
    for part in range(2):
        for i, j in IDX:
            for t in range(nt):
                raw[m, part, i, j, t, :, h * LANES : (h + 1) * LANES] = mat[part][i][j][t * nx : (t + 1) * nx]


def rotate_kernel(nt, nx, nh, time_links, space_links, rot, after, first, raw):
    tile = Tile(nt, nx, nh)
    for h in range(nh):
        here = load(rot, (), h)
        halo = load(first, (), h)
        beside = (
            load(after, (), h),
            each(lambda v, w: tile.x_up(v, tile.spread(w, nx - 1)), here, halo),
            each(tile.y_up, here, load(rot, (), (h + 1) % nh)),
            each(tile.z_up, here),
        )
        for m in range(4):
            links = load(time_links, (), h) if m == T else load(space_links, (m - 1,), h)
            put_raw(nt, nx, raw, m, h, mul(mul(here, links), beside[m], right_dag=True))


def call(kernel, outs, *args, scratch=()):
    where = [pl.BlockSpec(memory_space=pltpu.SMEM if arg.dtype == jnp.int32 else pltpu.VMEM) for arg in args]
    return pl.pallas_call(
        kernel,
        out_shape=[jax.ShapeDtypeStruct(shape, jnp.float32) for shape in outs],
        in_specs=where,
        out_specs=[pl.BlockSpec(memory_space=pltpu.VMEM)] * len(outs),
        scratch_shapes=[pltpu.VMEM(shape, jnp.float32) for shape in scratch],
    )(*args)


def body(raw):
    nt, nx, sites = raw.shape[4:]
    nh = sites // LANES
    tail = (nh, nt * nx, LANES)
    mat = (2, 3, 3)
    count_t, count_x = lax.axis_size("ta"), lax.axis_size("gx")

    def move(value, dt, dx, wrap=True):
        pairs = []
        for a in range(count_t):
            for b in range(count_x):
                if wrap or 0 <= a + dt < count_t:
                    pairs.append((a * count_x + b, (a + dt) % count_t * count_x + (b + dx) % count_x))
        return lax.ppermute(value, ("ta", "gx"), pairs)

    def halo(kept):
        lead = (2, kept, 3, nh)
        return [(3, *lead, nx, LANES), (3, *lead, nt, LANES), (*lead, 1, LANES), (*lead, 1, LANES)]

    def bind(kernel, *more):
        return functools.partial(kernel, nt, nx, nh, *more)

    site, *sent = call(bind(pack_kernel, 2), [(4, *mat, *tail), *halo(2)], raw)
    for kept in (2, 3):
        dt_in, dx_in = move(sent[0], -1, 0), move(sent[1], 0, -1)
        ct_in, cx_in = move(sent[2], 1, -1), move(sent[3], -1, 1)
        up_t, up_x, partial, corner, low = call(
            bind(early_kernel, kept),
            [*halo(kept)[:2], (4, *mat, *tail), (5, *mat, *tail), (4, *mat, *tail)],
            site,
            scratch=[(2, *mat, *tail)],
        )
        ut_in, ux_in = move(up_t, 1, 0), move(up_x, 0, 1)
        total, turn = call(
            bind(middle_kernel, kept),
            [(4, *mat, *tail), (2, *mat, *tail)],
            site, partial, corner, dt_in, dx_in,
            scratch=[(4, *mat, *tail)],
        )
        state = (site, total, turn, low, ut_in, ux_in, ct_in, cx_in)
        if kept == 2:
            site, *sent = call(bind(late_kernel, kept), [(4, *mat, *tail), *halo(3)], *state)
    time_links, product = call(bind(time_kernel, 3), [(*mat, *tail), (*mat, nh, nx, LANES)], *state)
    earlier = [move(product, step, 0, wrap=False) for step in range(1, count_t)]
    (space_links,) = call(bind(space_kernel, 3), [(3, *mat, *tail)], *state)
    mine = lax.axis_index("ta").astype(jnp.int32).reshape(1)
    rot, after, first = call(
        bind(gauge_kernel, count_t), [(*mat, *tail), (*mat, *tail), (*mat, nh, nt, LANES)], mine, time_links, *earlier
    )
    first_in = move(first, 0, -1)
    (out,) = call(bind(rotate_kernel), [raw.shape], time_links, space_links, rot, after, first_in)
    return out


def solution(mesh):
    spec = P(None, None, None, None, "ta", "gx", None)
    return jax.shard_map(body, mesh=mesh, in_specs=(spec,), out_specs=spec, check_vma=False)
```

```python
import functools

import jax
import jax.numpy as jnp
from jax import lax
from jax.experimental import pallas as pl
from jax.experimental.pallas import tpu as pltpu
from jax.sharding import PartitionSpec as P

NZ = 16
NEWTON = 5
LANES = 128
KEEP = 0.6
BLEND = 0.4 / 6.0
T, X, Y, Z = 0, 1, 2, 3
IDX = ((0, 0), (0, 1), (0, 2), (1, 0), (1, 1), (1, 2), (2, 0), (2, 1), (2, 2))
HALO_T = (X, Y, Z)
HALO_X = (T, Y, Z)


def load(ref, lead, h):
    return tuple([[ref[(*lead, part, i, j, h)] for j in range(3)] for i in range(3)] for part in range(2))


def store(ref, lead, h, mat):
    for part in range(2):
        for i, j in IDX:
            ref[(*lead, part, i, j, h)] = mat[part][i][j]


def accumulate(ref, lead, h, mat):
    for part in range(2):
        for i, j in IDX:
            ref[(*lead, part, i, j, h)] += mat[part][i][j]


def each(fn, *mats):
    return tuple([[fn(*[mat[part][i][j] for mat in mats]) for j in range(3)] for i in range(3)] for part in range(2))


def mul(left, right, left_dag=False, right_dag=False):
    out_re = [[None] * 3 for _ in range(3)]
    out_im = [[None] * 3 for _ in range(3)]
    for i, j in IDX:
        acc_re = acc_im = None
        for k in range(3):
            li, lj = (k, i) if left_dag else (i, k)
            ri, rj = (j, k) if right_dag else (k, j)
            a, b = left[0][li][lj], left[1][li][lj]
            c, d = right[0][ri][rj], right[1][ri][rj]
            ac, bd, ad, bc = a * c, b * d, a * d, b * c
            re = ac + bd if left_dag != right_dag else ac - bd
            if left_dag:
                im = ad - bc
            elif right_dag:
                im = bc - ad
            else:
                im = ad + bc
            acc_re = re if acc_re is None else acc_re + re
            acc_im = im if acc_im is None else acc_im + im
        out_re[i][j], out_im[i][j] = acc_re, acc_im
    return out_re, out_im


def third_row(mat):
    (re, im) = mat
    re, im = [re[0], re[1], [None] * 3], [im[0], im[1], [None] * 3]
    for j in range(3):
        u, v = (j + 1) % 3, (j + 2) % 3
        re[2][j] = re[0][u] * re[1][v] - im[0][u] * im[1][v] - re[0][v] * re[1][u] + im[0][v] * im[1][u]
        im[2][j] = re[0][v] * im[1][u] + im[0][v] * re[1][u] - re[0][u] * im[1][v] - im[0][u] * re[1][v]
    return re, im


class Tile:
    def __init__(self, nt, nx, nh):
        self.nt, self.nx, self.nh, self.rows = nt, nx, nh, nt * nx
        shape = (self.rows, LANES)
        self.row = lax.broadcasted_iota(jnp.int32, shape, 0)
        lane = lax.broadcasted_iota(jnp.int32, shape, 1)
        self.z_last = lane % NZ == NZ - 1
        self.z_first = lane % NZ == 0
        self.y_low = lane < LANES - NZ
        self.y_high = lane >= NZ

    def z_up(self, v):
        return jnp.where(self.z_last, pltpu.roll(v, NZ - 1, 1), pltpu.roll(v, LANES - 1, 1))

    def z_down(self, v):
        return jnp.where(self.z_first, pltpu.roll(v, LANES - NZ + 1, 1), pltpu.roll(v, 1, 1))

    def y_up(self, v, following):
        return jnp.where(self.y_low, pltpu.roll(v, LANES - NZ, 1), pltpu.roll(following, LANES - NZ, 1))

    def y_down(self, v, before):
        return jnp.where(self.y_high, pltpu.roll(v, NZ, 1), pltpu.roll(before, NZ, 1))

    def spread(self, halo, col):
        out = jnp.broadcast_to(halo[0:1], (self.rows, LANES))
        for t in range(1, self.nt):
            out = jnp.where(self.row >= t * self.nx, jnp.broadcast_to(halo[t : t + 1], (self.rows, LANES)), out)
        return out

    def col(self, x):
        return self.row % self.nx == x

    def x_up(self, v, halo):
        return jnp.where(self.col(self.nx - 1), halo, pltpu.roll(v, self.rows - 1, 0))

    def x_down(self, v, halo):
        return jnp.where(self.col(0), halo, pltpu.roll(v, 1, 0))

    def t_up(self, v, halo):
        return jnp.concatenate([v[self.nx :], halo], axis=0)

    def t_down(self, v, halo):
        return jnp.concatenate([halo, v[: self.rows - self.nx]], axis=0)

    def take_x(self, v, x):
        return jnp.concatenate([v[t * self.nx + x : t * self.nx + x + 1] for t in range(self.nt)], axis=0)


def up(tile, ref, m, k, h):
    here = load(ref, (m,), h)
    if k == Z:
        return each(tile.z_up, here)
    return each(tile.y_up, here, load(ref, (m,), (h + 1) % tile.nh))


def down(tile, ref, lead, k, h):
    here = load(ref, lead, h)
    if k == Z:
        return each(tile.z_down, here)
    return each(tile.y_down, here, load(ref, lead, (h + tile.nh - 1) % tile.nh))


def load_rows(ref, lead, h, kept):
    mat = tuple([[ref[(*lead, part, i, j, h)] for j in range(3)] for i in range(kept)] for part in range(2))
    return mat if kept == 3 else third_row(mat)


def store_rows(ref, lead, h, mat, kept):
    for part in range(2):
        for i in range(kept):
            for j in range(3):
                ref[(*lead, part, i, j, h)] = mat[part][i][j]


def send_down(tile, site, dt_ref, dx_ref, ct_ref, cx_ref, h, kept):
    nx, last = tile.nx, (tile.nt - 1) * tile.nx
    for m in range(4):
        mat = load(site, (m,), h)
        if m != T:
            store_rows(dt_ref, (m - 1,), h, each(lambda v: v[:nx], mat), kept)
        if m != X:
            store_rows(dx_ref, (HALO_X.index(m),), h, each(lambda v: tile.take_x(v, 0), mat), kept)
        if m == T:
            store_rows(ct_ref, (), h, each(lambda v: v[last : last + 1], mat), kept)
        if m == X:
            store_rows(cx_ref, (), h, each(lambda v: v[nx - 1 : nx], mat), kept)


def pack_kernel(nt, nx, nh, kept, raw, site, dt_ref, dx_ref, ct_ref, cx_ref):
    tile = Tile(nt, nx, nh)
    for h in range(nh):
        for m in range(4):
            for part in range(2):
                for i, j in IDX:
                    for t in range(nt):
                        site[m, part, i, j, h, t * nx : (t + 1) * nx] = raw[m, part, i, j, t, :, h * LANES : (h + 1) * LANES]
        send_down(tile, site, dt_ref, dx_ref, ct_ref, cx_ref, h, kept)


PAIRS = ((T, Y), (T, Z), (X, Y), (X, Z))


def early_kernel(nt, nx, nh, kept, site, ut_ref, ux_ref, part_ref, corner_ref, low_ref, low_yz):
    tile = Tile(nt, nx, nh)
    last = (nt - 1) * nx

    def step(h, _):
        u = functools.partial(load, site, h=h)
        y_of_z = up(tile, site, Z, Y, h)
        z_of_y = up(tile, site, Y, Z, h)
        path = mul(u((Y,)), y_of_z)
        other = mul(u((Z,)), z_of_y)
        store(part_ref, (Z,), h, mul(path, z_of_y, right_dag=True))
        store(part_ref, (Y,), h, mul(other, y_of_z, right_dag=True))
        store(low_yz, (0,), h, mul(u((Y,)), other, left_dag=True))
        store(low_yz, (1,), h, mul(u((Z,)), path, left_dag=True))
        for place, (k, m) in enumerate(PAIRS):
            other = mul(u((m,)), up(tile, site, k, m, h))
            store(corner_ref, (place,), h, other)
            low = mul(u((k,)), other, left_dag=True)
            store(low_ref, (place,), h, low)
            if k == T:
                store_rows(ut_ref, (m - 1,), h, each(lambda v: v[last:], low), kept)
            else:
                store_rows(ux_ref, (HALO_X.index(m),), h, each(lambda v: tile.take_x(v, nx - 1), low), kept)
        turn = mul(u((T,)), u((X,)), left_dag=True)
        store(corner_ref, (4,), h, turn)
        eye_x = tuple(
            [
                [
                    jnp.where(tile.col(nx - 1), 1.0 if part == 0 and i == j else 0.0, pltpu.roll(site[T, part, i, j, h], tile.rows - 1, 0))
                    for j in range(3)
                ]
                for i in range(3)
            ]
            for part in range(2)
        )
        low = mul(turn, eye_x)
        store_rows(ut_ref, (X - 1,), h, each(lambda v: v[last:], low), kept)
        eye_t = tuple(
            [
                [
                    jnp.where(tile.row >= last, 1.0 if part == 0 and i == j else 0.0, pltpu.roll(site[X, part, i, j, h], tile.rows - nx, 0))
                    for j in range(3)
                ]
                for i in range(3)
            ]
            for part in range(2)
        )
        low = mul(turn, eye_t, left_dag=True)
        store_rows(ux_ref, (HALO_X.index(T),), h, each(lambda v: tile.take_x(v, nx - 1), low), kept)
        return 0

    lax.fori_loop(0, nh, step, 0)

    def finish(h, _):
        accumulate(part_ref, (Z,), h, down(tile, low_yz, (0,), Y, h))
        accumulate(part_ref, (Y,), h, down(tile, low_yz, (1,), Z, h))
        return 0

    lax.fori_loop(0, nh, finish, 0)


def middle_kernel(nt, nx, nh, kept, site, part_ref, corner_ref, dt_ref, dx_ref, sum_ref, turn_ref, low_ref):
    tile = Tile(nt, nx, nh)

    def step(h, _):
        u = functools.partial(load, site, h=h)

        def ahead(m, k):
            if k == T:
                return each(tile.t_up, u((m,)), load_rows(dt_ref, (m - 1,), h, kept))
            halo = load_rows(dx_ref, (HALO_X.index(m),), h, kept)
            return each(lambda v, w: tile.x_up(v, tile.spread(w, nx - 1)), u((m,)), halo)

        x_of_t = ahead(T, X)
        t_of_x = ahead(X, T)
        store(sum_ref, (X,), h, mul(mul(u((T,)), t_of_x), x_of_t, right_dag=True))
        store(sum_ref, (T,), h, mul(mul(u((X,)), x_of_t), t_of_x, right_dag=True))
        turn = load(corner_ref, (4,), h)
        store(turn_ref, (0,), h, mul(turn, x_of_t))
        store(turn_ref, (1,), h, mul(turn, t_of_x, left_dag=True))
        for m in (Y, Z):
            store(sum_ref, (m,), h, load(part_ref, (m,), h))
        for place, (k, m) in enumerate(PAIRS):
            k_of_m = ahead(m, k)
            accumulate(sum_ref, (k,), h, mul(load(corner_ref, (place,), h), k_of_m, right_dag=True))
            path = mul(u((k,)), k_of_m)
            accumulate(sum_ref, (m,), h, mul(path, up(tile, site, k, m, h), right_dag=True))
            store(low_ref, (place,), h, mul(u((m,)), path, left_dag=True))
        return 0

    lax.fori_loop(0, nh, step, 0)

    def finish(h, _):
        for place, (k, m) in enumerate(PAIRS):
            accumulate(sum_ref, (k,), h, down(tile, low_ref, (place,), m, h))
        return 0

    lax.fori_loop(0, nh, finish, 0)


def unitarise(v):
    re, im = v
    diag = []
    for i in range(3):
        total = re[0][i] * re[0][i] + im[0][i] * im[0][i]
        for k in (1, 2):
            total = total + re[k][i] * re[k][i] + im[k][i] * im[k][i]
        diag.append(total)
    off = {}
    for i, j in ((0, 1), (0, 2), (1, 2)):
        off_re = re[0][i] * re[0][j] + im[0][i] * im[0][j]
        off_im = re[0][i] * im[0][j] - im[0][i] * re[0][j]
        for k in (1, 2):
            off_re = off_re + re[k][i] * re[k][j] + im[k][i] * im[k][j]
            off_im = off_im + re[k][i] * im[k][j] - im[k][i] * re[k][j]
        off[i, j] = (off_re, off_im)
    square = diag[0] + diag[1] + diag[2]
    bound = jnp.maximum(square, 1.0)
    inverse = lax.rsqrt(bound)
    inverse = inverse * (1.5 - 0.5 * bound * inverse * inverse)
    scale = inverse * inverse
    mean = square * scale * (1.0 / 3.0)
    q0, q1, q2 = (entry * scale - mean for entry in diag)
    ar, ai = (entry * scale for entry in off[0, 1])
    br, bi = (entry * scale for entry in off[0, 2])
    cr, ci = (entry * scale for entry in off[1, 2])
    na, nb, nc = ar * ar + ai * ai, br * br + bi * bi, cr * cr + ci * ci
    s0, s1, s2 = q0 * q0 + na + nb, q1 * q1 + na + nc, q2 * q2 + nb + nc
    sar, sai = br * cr + bi * ci - q2 * ar, bi * cr - br * ci - q2 * ai
    mr, mi = ar * cr - ai * ci, ar * ci + ai * cr
    sbr, sbi = mr - q1 * br, mi - q1 * bi
    scr, sci = ar * br + ai * bi - q0 * cr, ar * bi - ai * br - q0 * ci
    e2 = 0.5 * (s0 + s1 + s2)
    e3 = q0 * (q1 * q2 - nc) - q1 * nb - q2 * na + 2.0 * (mr * br + mi * bi)
    p0, p1, p2 = 1.5 - 0.5 * mean, jnp.full_like(mean, -0.5), jnp.zeros_like(mean)
    for _ in range(NEWTON - 1):
        d0, d1 = p0 + p0, p1 + p1
        t3, t4 = d1 * p2, p2 * p2
        z0 = p0 * p0 + e3 * t3
        z1 = d0 * p1 + e2 * t3 + e3 * t4
        z2 = p1 * p1 + d0 * p2 + e2 * t4
        y0 = 1.5 - 0.5 * (mean * z0 + e3 * z2)
        y1 = -0.5 * (mean * z1 + z0 + e2 * z2)
        y2 = -0.5 * (mean * z2 + z1)
        u3, u4 = p1 * y2 + p2 * y1, p2 * y2
        p0, p1, p2 = (
            p0 * y0 + e3 * u3,
            p0 * y1 + p1 * y0 + e2 * u3 + e3 * u4,
            p0 * y2 + p1 * y1 + p2 * y0 + e2 * u4,
        )
    p0, p1, p2 = p0 * inverse, p1 * inverse, p2 * inverse
    g0, g1, g2 = (p0 + p1 * q + p2 * s for q, s in ((q0, s0), (q1, s1), (q2, s2)))
    gar, gai = p1 * ar + p2 * sar, p1 * ai + p2 * sai
    gbr, gbi = p1 * br + p2 * sbr, p1 * bi + p2 * sbi
    gcr, gci = p1 * cr + p2 * scr, p1 * ci + p2 * sci
    out_re = [[None] * 3 for _ in range(3)]
    out_im = [[None] * 3 for _ in range(3)]
    for i in range(3):
        x0, x1, x2 = re[i]
        w0, w1, w2 = im[i]
        out_re[i][0] = x0 * g0 + x1 * gar + w1 * gai + x2 * gbr + w2 * gbi
        out_im[i][0] = w0 * g0 + w1 * gar - x1 * gai + w2 * gbr - x2 * gbi
        out_re[i][1] = x1 * g1 + x0 * gar - w0 * gai + x2 * gcr + w2 * gci
        out_im[i][1] = w1 * g1 + w0 * gar + x0 * gai + w2 * gcr - x2 * gci
        out_re[i][2] = x2 * g2 + x0 * gbr - w0 * gbi + x1 * gcr - w1 * gci
        out_im[i][2] = w2 * g2 + w0 * gbr + x0 * gbi + w1 * gcr + x1 * gci
    return out_re, out_im


def new_links(tile, kept, m, site, sum_ref, turn_ref, low_ref, ut_ref, ux_ref, ct_ref, cx_ref, h):
    nt, nx = tile.nt, tile.nx
    total = load(sum_ref, (m,), h)
    if m != T:
        source, lead = (turn_ref, (0,)) if m == X else (low_ref, (PAIRS.index((T, m)),))
        halo = load_rows(ut_ref, (m - 1,), h, kept)
        if m == X:
            end = mul(each(lambda v: v[nx - 1 :], halo), load_rows(ct_ref, (), h, kept))
            halo = each(lambda v, w: jnp.concatenate([v[: nx - 1], w], axis=0), halo, end)
        total = each(lambda acc, v, w: acc + tile.t_down(v, w), total, load(source, lead, h), halo)
    if m != X:
        source, lead = (turn_ref, (1,)) if m == T else (low_ref, (PAIRS.index((X, m)),))
        halo = load_rows(ux_ref, (HALO_X.index(m),), h, kept)
        if m == T:
            end = mul(each(lambda v: v[nt - 1 :], halo), load_rows(cx_ref, (), h, kept))
            halo = each(lambda v, w: jnp.concatenate([v[: nt - 1], w], axis=0), halo, end)
        total = each(lambda acc, v, w: acc + tile.x_down(v, tile.spread(w, 0)), total, load(source, lead, h), halo)
    return unitarise(each(lambda a, b: KEEP * a + BLEND * b, load(site, (m,), h), total))


def late_kernel(nt, nx, nh, kept, site, sum_ref, turn_ref, low_ref, ut_ref, ux_ref, ct_ref, cx_ref, out, dt_ref, dx_ref, dct_ref, dcx_ref):
    tile = Tile(nt, nx, nh)

    def step(h, _):
        for m in range(4):
            store(out, (m,), h, new_links(tile, kept, m, site, sum_ref, turn_ref, low_ref, ut_ref, ux_ref, ct_ref, cx_ref, h))
        send_down(tile, out, dt_ref, dx_ref, dct_ref, dcx_ref, h, 3)
        return 0

    lax.fori_loop(0, nh, step, 0)


def time_kernel(nt, nx, nh, kept, site, sum_ref, turn_ref, low_ref, ut_ref, ux_ref, ct_ref, cx_ref, out, prod_ref):
    tile = Tile(nt, nx, nh)

    def step(h, _):
        links = new_links(tile, kept, T, site, sum_ref, turn_ref, low_ref, ut_ref, ux_ref, ct_ref, cx_ref, h)
        store(out, (), h, links)
        run = each(lambda v: v[:nx], links)
        for t in range(1, nt):
            run = mul(run, each(lambda v: v[t * nx : (t + 1) * nx], links))
        store(prod_ref, (), h, run)
        return 0

    lax.fori_loop(0, nh, step, 0)


def space_kernel(nt, nx, nh, kept, site, sum_ref, turn_ref, low_ref, ut_ref, ux_ref, ct_ref, cx_ref, out):
    tile = Tile(nt, nx, nh)

    def step(h, _):
        for m in (X, Y, Z):
            store(out, (m - 1,), h, new_links(tile, kept, m, site, sum_ref, turn_ref, low_ref, ut_ref, ux_ref, ct_ref, cx_ref, h))
        return 0

    lax.fori_loop(0, nh, step, 0)


def gauge_kernel(nt, nx, nh, count, mine, links, *refs):
    earlier, (rot, after, first) = refs[: count - 1], refs[count - 1 :]
    tile = Tile(nt, nx, nh)
    me = mine[0]

    def step(h, _):
        run = None
        for place in reversed(range(count - 1)):
            there = jnp.full((nx, LANES), me, jnp.int32) > place
            mat = load(earlier[place], (), h)
            mat = tuple(
                [[jnp.where(there, mat[part][i][j], 1.0 if part == 0 and i == j else 0.0) for j in range(3)] for i in range(3)]
                for part in range(2)
            )
            run = mat if run is None else mul(run, mat)
        here = load(links, (), h)
        slices = [run]
        for t in range(nt):
            slices.append(mul(slices[-1], each(lambda v: v[t * nx : (t + 1) * nx], here)))
        before = each(lambda *v: jnp.concatenate(v, axis=0), *slices[:-1])
        store(rot, (), h, before)
        store(after, (), h, each(lambda *v: jnp.concatenate(v, axis=0), *slices[1:]))
        store(first, (), h, each(lambda v: tile.take_x(v, 0), before))
        return 0

    lax.fori_loop(0, nh, step, 0)


def put_raw(nt, nx, raw, m, h, mat):
    for part in range(2):
        for i, j in IDX:
            for t in range(nt):
                raw[m, part, i, j, t, :, h * LANES : (h + 1) * LANES] = mat[part][i][j][t * nx : (t + 1) * nx]


def rotate_kernel(nt, nx, nh, time_links, space_links, rot, after, first, raw):
    tile = Tile(nt, nx, nh)
    for h in range(nh):
        here = load(rot, (), h)
        halo = load(first, (), h)
        beside = (
            load(after, (), h),
            each(lambda v, w: tile.x_up(v, tile.spread(w, nx - 1)), here, halo),
            each(tile.y_up, here, load(rot, (), (h + 1) % nh)),
            each(tile.z_up, here),
        )
        for m in range(4):
            links = load(time_links, (), h) if m == T else load(space_links, (m - 1,), h)
            put_raw(nt, nx, raw, m, h, mul(mul(here, links), beside[m], right_dag=True))


def call(kernel, outs, *args, scratch=()):
    where = [pl.BlockSpec(memory_space=pltpu.SMEM if arg.dtype == jnp.int32 else pltpu.VMEM) for arg in args]
    return pl.pallas_call(
        kernel,
        out_shape=[jax.ShapeDtypeStruct(shape, jnp.float32) for shape in outs],
        in_specs=where,
        out_specs=[pl.BlockSpec(memory_space=pltpu.VMEM)] * len(outs),
        scratch_shapes=[pltpu.VMEM(shape, jnp.float32) for shape in scratch],
        compiler_params=pltpu.CompilerParams(vmem_limit_bytes=16 * 2**20),
    )(*args)


def body(raw):
    nt, nx, sites = raw.shape[4:]
    nh = sites // LANES
    tail = (nh, nt * nx, LANES)
    mat = (2, 3, 3)
    count_t, count_x = lax.axis_size("ta"), lax.axis_size("gx")

    def move(value, dt, dx, wrap=True):
        pairs = []
        for a in range(count_t):
            for b in range(count_x):
                if wrap or 0 <= a + dt < count_t:
                    pairs.append((a * count_x + b, (a + dt) % count_t * count_x + (b + dx) % count_x))
        return lax.ppermute(value, ("ta", "gx"), pairs)

    def halo(kept):
        lead = (2, kept, 3, nh)
        return [(3, *lead, nx, LANES), (3, *lead, nt, LANES), (*lead, 1, LANES), (*lead, 1, LANES)]

    def bind(kernel, *more):
        return functools.partial(kernel, nt, nx, nh, *more)

    site, *sent = call(bind(pack_kernel, 2), [(4, *mat, *tail), *halo(2)], raw)
    for kept in (2, 3):
        dt_in, dx_in = move(sent[0], -1, 0), move(sent[1], 0, -1)
        ct_in, cx_in = move(sent[2], 1, -1), move(sent[3], -1, 1)
        up_t, up_x, partial, corner, low = call(
            bind(early_kernel, kept),
            [*halo(kept)[:2], (4, *mat, *tail), (5, *mat, *tail), (4, *mat, *tail)],
            site,
            scratch=[(2, *mat, *tail)],
        )
        ut_in, ux_in = move(up_t, 1, 0), move(up_x, 0, 1)
        total, turn = call(
            bind(middle_kernel, kept),
            [(4, *mat, *tail), (2, *mat, *tail)],
            site, partial, corner, dt_in, dx_in,
            scratch=[(4, *mat, *tail)],
        )
        state = (site, total, turn, low, ut_in, ux_in, ct_in, cx_in)
        if kept == 2:
            site, *sent = call(bind(late_kernel, kept), [(4, *mat, *tail), *halo(3)], *state)
    time_links, product = call(bind(time_kernel, 3), [(*mat, *tail), (*mat, nh, nx, LANES)], *state)
    earlier = [move(product, step, 0, wrap=False) for step in range(1, count_t)]
    (space_links,) = call(bind(space_kernel, 3), [(3, *mat, *tail)], *state)
    mine = lax.axis_index("ta").astype(jnp.int32).reshape(1)
    rot, after, first = call(
        bind(gauge_kernel, count_t), [(*mat, *tail), (*mat, *tail), (*mat, nh, nt, LANES)], mine, time_links, *earlier
    )
    first_in = move(first, 0, -1)
    (out,) = call(bind(rotate_kernel), [raw.shape], time_links, space_links, rot, after, first_in)
    return out


def solution(mesh):
    spec = P(None, None, None, None, "ta", "gx", None)
    return jax.shard_map(body, mesh=mesh, in_specs=(spec,), out_specs=spec, check_vma=False)
```
